128 devices in a mesh: sy: 4 (over y_lo, core), sx: 4 (over x), ch: 8 (over z, y_hi).
Axes of the slice: x: 4, y: 4 (y_hi: 2, y_lo: 2; y = y_hi * 2 + y_lo), z: 4, core: 2. Of those that a mesh axis runs over, the one named last changes fastest.
Arguments:
- frames: bfloat16 [144, 144, 128], P('sy', 'sx'), may hold values from -6 to 6
- w_input: bfloat16 [9, 64, 4, 1024], P(None, None, None, 'ch'), may hold values from -0.25 to 0.25
- w_hidden: bfloat16 [9, 1024, 4, 1024], P(None, None, None, 'ch'), may hold values from -0.0625 to 0.0625
- biases: float32 [4, 1024], P(None, 'ch'), may hold values from -4 to 4
- hidden_init: bfloat16 [144, 144, 1024], P('sy', 'sx', 'ch'), may hold values from -1 to 1
- cell_init: float32 [144, 144, 1024], P('sy', 'sx', 'ch'), may hold values from -5 to 5
Outputs:
- hidden_out: bfloat16 [144, 144, 1024], P('sy', 'sx', 'ch')
- cell_out: float32 [144, 144, 1024], P('sy', 'sx', 'ch')
The draws below stay inside these ranges and needn't reach their ends.
All inputs are finite; a program needn't handle non-finite values.
Results may differ from the reference program's by a relative error of at most 0.0021.
Values may be sent and summed in bfloat16 or wider, within the bound.
A program may use at most 192 MiB of HBM per device.

```python
import jax
import jax.numpy as jnp
from jax import lax

HID = 1024
CIN = 64
STEPS = 2
NY = 144
NX = 144


def level_of(key, shape, shards, low, largest):
    loudness = 1.0
    for dim, shards_of in shards:
        heights = jax.random.uniform(jax.random.fold_in(jax.random.fold_in(key, 6), dim), (shards_of,), jnp.float32, low / len(shards), largest / len(shards))
        loudness = loudness * jnp.repeat(jnp.exp(heights), shape[dim] // shards_of).reshape((-1,) + (1,) * (len(shape) - 1 - dim))
    return loudness


def gaussian(stream_key, extent, deviation, reach, cuts=(), kind=jnp.bfloat16):
    drawn = jax.random.normal(stream_key, extent, jnp.float32) * deviation
    if len(cuts) > 0:
        drawn = level_of(stream_key, extent, cuts, -0.22, 0.18) * drawn
    return jnp.clip(drawn, min=-reach, max=reach).astype(kind)


def setup_inputs(seed: int = 0) -> dict:
    key_of = jax.random.split(jax.random.key(seed), 7)
    frames = gaussian(key_of[0], (NY, NX, STEPS * CIN), 1.0, 6.0, ((0, 4), (1, 4)))
    w_input = gaussian(key_of[1], (9, CIN, 4, HID), (9 * CIN) ** -0.5, 0.25, ((3, 8),))
    w_hidden = gaussian(key_of[2], (9, HID, 4, HID), (9 * HID) ** -0.5, 0.0625, ((3, 8),))
    biases = gaussian(key_of[3], (4, HID), 1.0, 4.0, ((1, 8),), jnp.float32)
    hidden_init = jnp.clip(jax.random.uniform(key_of[4], (NY, NX, HID), jnp.float32, -1.0, 1.0) * level_of(key_of[4], (NY, NX, HID), ((0, 4), (1, 4), (2, 8)), -0.4, 0.0), -1.0, 1.0).astype(jnp.bfloat16)
    cell_init = gaussian(key_of[5], (NY, NX, HID), 1.0, 5.0, ((0, 4), (1, 4), (2, 8)), jnp.float32)
    return {"frames": frames, "w_input": w_input, "w_hidden": w_hidden, "biases": biases, "hidden_init": hidden_init, "cell_init": cell_init}


def convolve(field, kernels):
    channels = field.shape[-1]
    rhs = kernels.astype(jnp.float32).reshape(3, 3, channels, -1)
    out = lax.conv_general_dilated(field.astype(jnp.float32)[None], rhs, (1, 1), "SAME", dimension_numbers=("NHWC", "HWIO", "NHWC"))
    return out[0]


def reference(frames, w_input, w_hidden, biases, hidden_init, cell_init):
    hidden = hidden_init
    cell = cell_init
    rows, cols = hidden.shape[0], hidden.shape[1]
    for step in range(STEPS):
        frame = frames[:, :, step * CIN:(step + 1) * CIN]
        pre = convolve(frame, w_input) + convolve(hidden, w_hidden)
        pre = pre.reshape(rows, cols, 4, HID) + biases[None, None]
        cell = jax.nn.sigmoid(pre[:, :, 1]) * cell + jax.nn.sigmoid(pre[:, :, 0]) * jnp.tanh(pre[:, :, 3])
        hidden = (jax.nn.sigmoid(pre[:, :, 2]) * jnp.tanh(cell)).astype(jnp.bfloat16)
    return hidden, cell
```

```python
import functools

import jax
import jax.numpy as jnp
from jax import lax
from jax.experimental import pallas as pl
from jax.experimental.pallas import tpu as pltpu
from jax.sharding import PartitionSpec as P

F32 = jnp.float32
BF = jnp.bfloat16
MESH = pl.DeviceIdType.MESH

ROWS = 36
PITCH = ROWS + 2
PAD_ROWS = 1456
OUT_ROWS = 1376
SENT = (800, 752)
DONE = (720, 672)
TILES = ((144, 328), (168, 176))
TAPS = [dy * PITCH + dx for dy in range(3) for dx in range(3)]
HALO = [(dy, dx) for dy in (-1, 0, 1) for dx in (-1, 0, 1) if (dy, dx) != (0, 0)]
STRIP = 48


def sigmoid(x):
    return 0.5 * jnp.tanh(0.5 * x) + 0.5


def kernel(
    frames, w_in, w_hid, bias_in, hid_in, cell_in, hid_out, cell_out,
    fr_v, hid_v, cell_v, bias_v, raw_in, raw, wts, wts_in, spread,
    hid_p, fr_p, fr_pair, gathered, window, total, cell, strip_out, strip_in,
    hid_o, cell_o,
    load_sem, halo_send, halo_recv, send_sem, recv_sem, store_sem,
):
    sy, sx, ch = lax.axis_index("sy"), lax.axis_index("sx"), lax.axis_index("ch")
    z, half = ch // 2, ch % 2
    odd = sy % 2
    turn = 1 - 2 * odd

    def y_of(r):
        return r + odd * (ROWS - 1 - 2 * r)

    def at(dy=0, dx=0, dz=0, other=0):
        return (
            lax.rem(sy + dy * turn + 4, 4),
            lax.rem(sx + dx + 4, 4),
            lax.rem(z + dz + 4, 4) * 2 + lax.rem(half + other, 2),
        )

    def load(source, target, k):
        return pltpu.make_async_copy(source, target, load_sem.at[k])

    places = [(0, 0), (0, 1), (1, 0), (3, 0), (1, 1), (3, 1), (2, 0), (2, 1)]
    loads = [
        load(hid_in, hid_v, 0), load(frames, fr_v, 1), load(w_in, raw_in, 2),
    ]
    for j, (dz, other) in enumerate(places):
        c = lax.rem(z + dz, 4) * 2 + lax.rem(half + other, 2)
        first = pl.multiple_of(c * 512, 512)
        loads.append(load(w_hid.at[:, pl.ds(first, 512)], raw.at[j], 3 + j))
    loads += [load(cell_in, cell_v, 11), load(bias_in, bias_v, 12)]
    for copy in loads:
        copy.start()

    partners = [at(dy, dx) for dy, dx in HALO] + [at(dz=1), at(dz=-1), at(other=1)]
    barrier = pltpu.get_barrier_semaphore()
    for partner in partners:
        pl.semaphore_signal(barrier, inc=1, device_id=partner, device_id_type=MESH)

    for ref in (hid_p, fr_p):
        ref[pl.ds(0, 40), :] = jnp.zeros((40, 128), F32)
        ref[pl.ds(1400, PAD_ROWS + 8 - 1400), :] = jnp.zeros((PAD_ROWS + 8 - 1400, 128), F32)
    loads[0].wait()
    for y in range(ROWS):
        hid_p[pl.ds(PITCH * (y + 1) + 1, ROWS), :] = hid_v[y_of(y)].astype(F32)
    loads[1].wait()
    for y in range(ROWS):
        fr_p[pl.ds(PITCH * (y + 1) + 1, ROWS), :] = fr_v[y_of(y)].astype(F32)

    def edge(dy, dx, lo, hi, mine):
        def pick(d):
            if mine:
                return {-1: 1, 1: ROWS}[d]
            return {-1: 0, 1: ROWS + 1}[d]

        if dy == 0:
            return (lo + 1) * PITCH + pick(dx), hi - lo, PITCH
        if dx == 0:
            return pick(dy) * PITCH + 1, ROWS, 1
        return pick(dy) * PITCH + pick(dx), 1, 1

    def rows_of(ref, first, count, stride):
        if stride == 1:
            return ref.at[pl.ds(first, count), :]
        return ref.at[pl.ds(first, count, stride=stride), :]

    def halo_copy(e, k, there):
        dy, dx = HALO[k]
        part = (pl.ds(0, 2 if e == 0 else 1), pl.ds(0, STRIP if dy == 0 or dx == 0 else 16))
        source, target = (HALO.index((dy, -dx)), k) if there else (k, HALO.index((dy, -dx)))
        return pltpu.make_async_remote_copy(
            src_ref=strip_out.at[(e, source) + part],
            dst_ref=strip_in.at[(e, target) + part],
            send_sem=halo_send.at[e, source],
            recv_sem=halo_recv.at[e, target],
            device_id=at(dy, dx),
            device_id_type=MESH,
        )

    def sides(band):
        return [
            k for k, (dy, _) in enumerate(HALO)
            if band is None or dy == 0 or (dy == -1) == (band == 0)
        ]

    def column(band):
        return {None: (0, ROWS), 0: (0, 19), 1: (18, ROWS)}[band]

    def halo_start(e, band, fields):
        lo, hi = column(band)
        for k in sides(band):
            dy, dx = HALO[k]
            first, count, stride = edge(dy, dx, lo, hi, True)
            for f, ref in enumerate(fields):
                strip_out[e, k, f, pl.ds(0, count), :] = rows_of(ref, first, count, stride)[...].astype(BF)
            halo_copy(e, k, False).start()

    def halo_finish(e, band, fields):
        lo, hi = column(band)
        for k in sides(band):
            dy, dx = HALO[k]
            halo_copy(e, k, True).wait_recv()
            inside = jnp.where(
                ((sy + dy * turn >= 0) & (sy + dy * turn < 4)) & ((sx + dx >= 0) & (sx + dx < 4)), 1.0, 0.0
            ).astype(F32)
            first, count, stride = edge(dy, dx, lo, hi, False)
            for f, ref in enumerate(fields):
                got = strip_in[e, k, f, pl.ds(0, count), :].astype(F32) * inside
                rows_of(ref, first, count, stride)[...] = got

    def bounds(s, b):
        lo, hi = ((0, SENT[s]), (SENT[s], PAD_ROWS))[b]
        middle = lo + (hi - lo) // 32 * 16
        return lo, middle, hi

    def piece(s, b, i):
        lo, middle, hi = bounds(s, b)
        whole, one, two = (lo, hi - lo), (lo, middle - lo), (middle, hi - middle)
        up, down, across = at(dz=1), at(dz=-1), at(other=1)
        return [
            (0, 1, whole, across),
            (0, 3, whole, up),
            (0, 2, whole, down),
            (3, 6, one, up),
            (2, 6, two, down),
            (1, 5, whole, up),
            (1, 4, whole, down),
            (6, 7, one, across),
            (6, 7, two, across),
        ][i]

    def gather_copy(s, b, i):
        here, there, (first, count), target = piece(s, b, i)
        return pltpu.make_async_remote_copy(
            src_ref=gathered.at[s, here, pl.ds(first, count)],
            dst_ref=gathered.at[s, there, pl.ds(first, count)],
            send_sem=send_sem.at[s, b, i],
            recv_sem=recv_sem.at[s, b, i],
            device_id=target,
            device_id_type=MESH,
        )

    def send(s, b, *pieces):
        for i in pieces:
            gather_copy(s, b, i).start()

    def arrived(s, b, *pieces):
        for i in pieces:
            gather_copy(s, b, i).wait_recv()

    def own_band(s, b):
        lo, _, hi = bounds(s, b)
        gathered[s, 0, pl.ds(lo, hi - lo), :] = hid_p[pl.ds(lo, hi - lo), :].astype(BF)
        send(s, b, 1, 2, 0)

    def event(s, b, n):
        if n == 0:
            arrived(s, b, 1, 2)
            send(s, b, 3, 4)
            arrived(s, b, 0)
            send(s, b, 5, 6)
        elif n == 1:
            arrived(s, b, 3, 4)
            send(s, b, 7, 8)
        elif n == 2:
            arrived(s, b, 5, 6)
        elif n == 3:
            arrived(s, b, 7, 8)

    def relay(q):
        def unit(u, _):
            tap = u % 9
            spread[...] = raw[2 * q + u // 9, tap + odd * (6 - 6 * (tap // 3))].astype(F32)
            for g in range(4):
                wts[q, pl.ds(pl.multiple_of(u * 128, 128), 128), pl.ds(g * 128, 128)] = spread[
                    pl.ds(g, 128, stride=4), :
                ].astype(BF)
            return 0

        lax.fori_loop(0, 18, unit, 0)

    def relay_input():
        for dy in range(3):
            for dx in range(3):
                spread[pl.ds(0, 256), :] = raw_in[3 * (dy + odd * (2 - 2 * dy)) + dx].astype(F32)
                for g in range(4):
                    wts_in[pl.ds(dy * 256 + dx * 64, 64), pl.ds(g * 128, 128)] = spread[
                        pl.ds(g, 64, stride=4), :
                    ].astype(BF)
            wts_in[pl.ds(dy * 256 + 192, 64), :] = jnp.zeros((64, 512), BF)

    def frames_part(s, b):
        lo, count = ((0, DONE[s]), (DONE[s], OUT_ROWS - DONE[s]))[b]
        lhs = jnp.concatenate(
            [
                fr_pair[s, pl.ds(lo + dy * PITCH + dx, count), :].astype(BF)
                for dy in range(3)
                for dx in (0, 2)
            ],
            axis=1,
        )
        total[pl.ds(lo, count), :] = jnp.dot(lhs, wts_in[...], preferred_element_type=F32)

    def hidden_part(s, b, q):
        lo, count = ((0, DONE[s]), (DONE[s], OUT_ROWS - DONE[s]))[b]
        reach = (SENT[s], PAD_ROWS - DONE[s])[b]
        for p in range(2):
            window[p, pl.ds(0, reach), :] = gathered[s, 2 * q + p, pl.ds(lo, reach), :].astype(F32)
        lhs = jnp.concatenate(
            [window[p, pl.ds(tap, count), :].astype(BF) for p in range(2) for tap in TAPS], axis=1
        )
        total[pl.ds(lo, count), :] += jnp.dot(lhs, wts[q], preferred_element_type=F32)

    def gates_part(s, b):
        lo, count = ((0, DONE[s]), (DONE[s], OUT_ROWS - DONE[s]))[b]
        tile = TILES[s][b]

        def one(i, _):
            first = pl.multiple_of(lo + i * tile, 8)
            gate = [
                total[pl.ds(first, tile), pl.ds(g * 128, 128)] + bias_v[pl.ds(g, 1), :]
                for g in range(4)
            ]
            new = sigmoid(gate[1]) * cell[pl.ds(first, tile), :] + sigmoid(gate[0]) * jnp.tanh(gate[3])
            cell[pl.ds(first, tile), :] = new
            hid_p[pl.ds(first + PITCH + 1, tile), :] = sigmoid(gate[2]) * jnp.tanh(new)
            return 0

        lax.fori_loop(0, count // tile, one, 0)

    both = (hid_p, fr_p)
    pl.semaphore_wait(barrier, len(partners))
    halo_start(0, None, both)
    loads[2].wait()
    relay_input()
    halo_finish(0, None, both)
    own_band(0, 0)
    own_band(0, 1)

    lane = lax.broadcasted_iota(jnp.int32, (104, 128), 1)

    def pair_up(i, _):
        first = pl.multiple_of(i * 104, 8)
        here = fr_p[pl.ds(first, 104), :]
        there = fr_p[pl.ds(first + 1, 104), :]
        fr_pair[0, pl.ds(first, 104), :] = jnp.where(lane < 64, here, pltpu.roll(there, 64, 1))
        fr_pair[1, pl.ds(first, 104), :] = jnp.where(lane < 64, pltpu.roll(here, 64, 1), there)
        return 0

    lax.fori_loop(0, PAD_ROWS // 104, pair_up, 0)

    cell[...] = jnp.zeros_like(cell)
    loads[11].wait()
    loads[12].wait()
    for y in range(ROWS):
        cell[pl.ds(PITCH * y, ROWS), :] = cell_v[y_of(y)]
    for j in range(8):
        loads[3 + j].wait()
    for q in range(4):
        relay(q)

    def band(s, b, before):
        frames_part(s, b)

        def part(q, _):
            for n in range(4):
                @pl.when(q == n)
                def _():
                    for act in before[n]:
                        act()
            hidden_part(s, b, q)
            return 0

        lax.fori_loop(0, 4, part, 0)
        gates_part(s, b)

    def ev(s, b, n):
        return functools.partial(event, s, b, n)

    def next_band(b):
        halo_start(1 + b, b, (hid_p,))

    def next_out(b):
        halo_finish(1 + b, b, (hid_p,))
        own_band(1, b)

    nothing = ()
    band(0, 0, [[ev(0, 0, 0)], [], [ev(0, 0, 1), ev(0, 1, 0), ev(0, 0, 2)], [ev(0, 0, 3)]])
    next_band(0)
    band(0, 1, [
        [ev(0, 1, 1)], [functools.partial(next_out, 0)], [ev(0, 1, 2)], [ev(0, 1, 3)],
    ])
    next_band(1)
    next_out(1)
    band(1, 0, [[ev(1, 0, 0)], [], [ev(1, 0, 1), ev(1, 1, 0), ev(1, 0, 2)], [ev(1, 0, 3)]])

    def finish(first, last):
        for r in range(first, last):
            hid_o[y_of(r)] = hid_p[pl.ds(PITCH * (r + 1) + 1, ROWS), :].astype(BF)
            cell_o[y_of(r)] = cell[pl.ds(PITCH * r, ROWS), :]
        rows = pl.ds(first + odd * (ROWS - last - first), last - first)
        k = int(first > 0)
        copies = [
            pltpu.make_async_copy(hid_o.at[rows], hid_out.at[rows], store_sem.at[0, k]),
            pltpu.make_async_copy(cell_o.at[rows], cell_out.at[rows], store_sem.at[1, k]),
        ]
        for copy in copies:
            copy.start()
        return copies

    ends = finish(0, 17)
    band(1, 1, [[ev(1, 1, 1)], [], [ev(1, 1, 2)], [ev(1, 1, 3)]])
    ends += finish(17, ROWS)

    for k in range(8):
        halo_copy(0, k, False).wait_send()
    for b in range(2):
        for k in sides(b):
            halo_copy(1 + b, k, False).wait_send()
    for s in range(2):
        for b in range(2):
            for i in range(9):
                gather_copy(s, b, i).wait_send()
    for copy in ends:
        copy.wait()


def per_device(frames, w_input, w_hidden, biases, hidden_init, cell_init):
    w_in = w_input.reshape(9, 256, 128)
    w_hid = w_hidden.reshape(9, 4096, 128)
    dma = pltpu.SemaphoreType.DMA
    return pl.pallas_call(
        kernel,
        out_shape=(
            jax.ShapeDtypeStruct((ROWS, ROWS, 128), BF),
            jax.ShapeDtypeStruct((ROWS, ROWS, 128), F32),
        ),
        in_specs=[pl.BlockSpec(memory_space=pl.ANY)] * 6,
        out_specs=(pl.BlockSpec(memory_space=pl.ANY),) * 2,
        scratch_shapes=[
            pltpu.VMEM((ROWS, ROWS, 128), BF),
            pltpu.VMEM((ROWS, ROWS, 128), BF),
            pltpu.VMEM((ROWS, ROWS, 128), F32),
            pltpu.VMEM((4, 128), F32),
            pltpu.VMEM((9, 256, 128), BF),
            pltpu.VMEM((8, 9, 512, 128), BF),
            pltpu.VMEM((4, 2304, 512), BF),
            pltpu.VMEM((768, 512), BF),
            pltpu.VMEM((512, 128), F32),
            pltpu.VMEM((PAD_ROWS + 8, 128), F32),
            pltpu.VMEM((PAD_ROWS + 8, 128), F32),
            pltpu.VMEM((2, PAD_ROWS, 128), F32),
            pltpu.VMEM((2, 8, PAD_ROWS, 128), BF),
            pltpu.VMEM((2, SENT[0], 128), F32),
            pltpu.VMEM((OUT_ROWS, 512), F32),
            pltpu.VMEM((OUT_ROWS, 128), F32),
            pltpu.VMEM((3, 8, 2, STRIP, 128), BF),
            pltpu.VMEM((3, 8, 2, STRIP, 128), BF),
            pltpu.VMEM((ROWS, ROWS, 128), BF),
            pltpu.VMEM((ROWS, ROWS, 128), F32),
            dma((13,)),
            dma((3, 8)),
            dma((3, 8)),
            dma((2, 2, 9)),
            dma((2, 2, 9)),
            dma((2, 2)),
        ],
        compiler_params=pltpu.CompilerParams(
            collective_id=0, has_side_effects=True, vmem_limit_bytes=60 * 1024 * 1024
        ),
        name="conv_lstm",
    )(frames, w_in, w_hid, biases, hidden_init, cell_init)


def solution(mesh):
    in_specs = (
        P("sy", "sx", None),
        P(None, None, None, "ch"),
        P(None, None, None, "ch"),
        P(None, "ch"),
        P("sy", "sx", "ch"),
        P("sy", "sx", "ch"),
    )
    out_specs = (P("sy", "sx", "ch"), P("sy", "sx", "ch"))
    return jax.shard_map(
        per_device, mesh=mesh, in_specs=in_specs, out_specs=out_specs, check_vma=False
    )
```

```python
import functools

import jax
import jax.numpy as jnp
from jax import lax
from jax.experimental import pallas as pl
from jax.experimental.pallas import tpu as pltpu
from jax.sharding import PartitionSpec as P

F32 = jnp.float32
BF = jnp.bfloat16
MESH = pl.DeviceIdType.MESH

ROWS = 36
PITCH = ROWS + 2
PAD_ROWS = 1456
OUT_ROWS = 1376
SENT = (800, 752)
DONE = (720, 672)
TILES = ((144, 328), (168, 176))
TAPS = [dy * PITCH + dx for dy in range(3) for dx in range(3)]
HALO = [(dy, dx) for dy in (-1, 0, 1) for dx in (-1, 0, 1) if (dy, dx) != (0, 0)]
STRIP = 48
CELLS = 20
TAIL = (128, 112)


def sigmoid(x):
    return 0.5 * jnp.tanh(0.5 * x) + 0.5


def kernel(
    frames, w_in, w_hid, bias_in, hid_in, cell_in, hid_out, cell_out,
    fr_v, hid_v, cell_v, bias_v, raw_in, raw, wts, wts_in, spread,
    hid_p, fr_p, fr_pair, gathered, window, total, cell, strip_out, strip_in,
    hid_f, packs, pack_f,
    load_sem, halo_send, halo_recv, send_sem, recv_sem, pack_send, pack_recv, store_sem,
):
    sy, sx, ch = lax.axis_index("sy"), lax.axis_index("sx"), lax.axis_index("ch")
    z, half = ch // 2, ch % 2
    odd = sy % 2
    turn = 1 - 2 * odd

    def y_of(r):
        return r + odd * (ROWS - 1 - 2 * r)

    def at(dy=0, dx=0, dz=0, other=0):
        return (
            lax.rem(sy + dy * turn + 4, 4),
            lax.rem(sx + dx + 4, 4),
            lax.rem(z + dz + 4, 4) * 2 + lax.rem(half + other, 2),
        )

    def load(source, target, k):
        return pltpu.make_async_copy(source, target, load_sem.at[k])

    places = [(0, 0), (0, 1), (1, 0), (3, 0), (1, 1), (3, 1), (2, 0), (2, 1)]
    loads = [
        load(hid_in, hid_v, 0), load(frames, fr_v, 1), load(w_in, raw_in, 2),
    ]
    for j, (dz, other) in enumerate(places):
        c = lax.rem(z + dz, 4) * 2 + lax.rem(half + other, 2)
        first = pl.multiple_of(c * 512, 512)
        loads.append(load(w_hid.at[:, pl.ds(first, 512)], raw.at[j], 3 + j))
    loads += [load(cell_in, cell_v, 11), load(bias_in, bias_v, 12)]
    for copy in loads:
        copy.start()

    partners = [at(dy, dx) for dy, dx in HALO] + [at(dz=1), at(dz=-1), at(other=1)]
    barrier = pltpu.get_barrier_semaphore()
    for partner in partners:
        pl.semaphore_signal(barrier, inc=1, device_id=partner, device_id_type=MESH)

    for ref in (hid_p, fr_p):
        ref[...] = jnp.zeros_like(ref)
    loads[0].wait()
    for y in range(ROWS):
        hid_p[pl.ds(PITCH * (y + 1) + 1, ROWS), :] = hid_v[y_of(y)].astype(F32)
    loads[1].wait()
    for y in range(ROWS):
        fr_p[pl.ds(PITCH * (y + 1) + 1, ROWS), :] = fr_v[y_of(y)].astype(F32)

    def edge(dy, dx, lo, hi, mine):
        def pick(d):
            if mine:
                return {-1: 1, 1: ROWS}[d]
            return {-1: 0, 1: ROWS + 1}[d]

        if dy == 0:
            return (lo + 1) * PITCH + pick(dx), hi - lo, PITCH
        if dx == 0:
            return pick(dy) * PITCH + 1, ROWS, 1
        return pick(dy) * PITCH + pick(dx), 1, 1

    def rows_of(ref, first, count, stride):
        if stride == 1:
            return ref.at[pl.ds(first, count), :]
        return ref.at[pl.ds(first, count, stride=stride), :]

    def halo_copy(e, k, there):
        dy, dx = HALO[k]
        part = (pl.ds(0, 2 if e == 0 else 1), pl.ds(0, STRIP if dy == 0 or dx == 0 else 16))
        source, target = (HALO.index((dy, -dx)), k) if there else (k, HALO.index((dy, -dx)))
        return pltpu.make_async_remote_copy(
            src_ref=strip_out.at[(e, source) + part],
            dst_ref=strip_in.at[(e, target) + part],
            send_sem=halo_send.at[e, source],
            recv_sem=halo_recv.at[e, target],
            device_id=at(dy, dx),
            device_id_type=MESH,
        )

    def sides(band):
        return [
            k for k, (dy, _) in enumerate(HALO)
            if band is None or dy == 0 or (dy == -1) == (band == 0)
        ]

    def column(band):
        return {None: (0, ROWS), 0: (0, CELLS), 1: (ROWS - CELLS, ROWS)}[band]

    def halo_fill(e, band, fields):
        lo, hi = column(band)
        for k in sides(band):
            dy, dx = HALO[k]
            first, count, stride = edge(dy, dx, lo, hi, True)
            for f, ref in enumerate(fields):
                strip_out[e, k, f, pl.ds(0, count), :] = rows_of(ref, first, count, stride)[...].astype(BF)

    def halo_start(e, band):
        for k in sides(band):
            halo_copy(e, k, False).start()

    def inside(k):
        dy, dx = HALO[k]
        ok = ((sy + dy * turn >= 0) & (sy + dy * turn < 4)) & ((sx + dx >= 0) & (sx + dx < 4))
        return jnp.where(ok, 1.0, 0.0).astype(F32)

    def halo_finish(e, s, band):
        for k in sides(band):
            halo_copy(e, k, True).wait_recv()
        for b in (0, 1) if band is None else (band,):
            skip = 0 if band is not None else column(b)[0]

            def got(dy, dx, first, count):
                k = HALO.index((dy, dx))
                return strip_in[e, k, 0, pl.ds(first, count), :].astype(F32) * inside(k)

            edge_dy = 2 * b - 1
            pack_f[0, pl.ds(0, CELLS), :] = got(0, -1, skip, CELLS)
            pack_f[0, pl.ds(CELLS, CELLS), :] = got(0, 1, skip, CELLS)
            pack_f[0, pl.ds(2 * CELLS, 1), :] = got(edge_dy, -1, 0, 1)
            pack_f[0, pl.ds(2 * CELLS + 1, ROWS), :] = got(edge_dy, 0, 0, ROWS)
            pack_f[0, pl.ds(2 * CELLS + 1 + ROWS, 1), :] = got(edge_dy, 1, 0, 1)
            packs[s, 0, b] = pack_f[0].astype(BF)

    def frames_halo():
        for k, (dy, dx) in enumerate(HALO):
            first, count, stride = edge(dy, dx, 0, ROWS, False)
            rows_of(fr_p, first, count, stride)[...] = (
                strip_in[0, k, 1, pl.ds(0, count), :].astype(F32) * inside(k)
            )

    def bounds(s, b):
        lo, hi = ((32, SENT[s]), (SENT[s], 1408))[b]
        middle = lo + (hi - lo) // 32 * 16
        return lo, middle, hi

    def piece(s, b, i):
        lo, middle, hi = bounds(s, b)
        cut = hi - TAIL[b]
        one, two = (lo, middle - lo), (middle, hi - middle)
        most, tail = (lo, cut - lo), (cut, hi - cut)
        up, down, across = at(dz=1), at(dz=-1), at(other=1)
        return [
            (0, 1, one, across), (0, 3, one, up), (0, 2, one, down),
            (0, 1, two, across), (0, 3, two, up), (0, 2, two, down),
            (3, 6, one, up), (2, 6, two, down),
            (1, 5, most, up), (1, 4, most, down), (2, 4, tail, across), (3, 5, tail, across),
            (6, 7, one, across), (6, 7, two, across),
        ][i]

    FIRST, SECOND, AHEAD, ROUND, TAILS, CROSS = (1, 2, 0), (4, 5, 3), (6, 7), (8, 9), (10, 11), (12, 13)

    def gather_copy(s, b, i):
        here, there, (first, count), target = piece(s, b, i)
        return pltpu.make_async_remote_copy(
            src_ref=gathered.at[s, here, pl.ds(first, count)],
            dst_ref=gathered.at[s, there, pl.ds(first, count)],
            send_sem=send_sem.at[s, b, i],
            recv_sem=recv_sem.at[s, b, i],
            device_id=target,
            device_id_type=MESH,
        )

    def send(s, b, *groups):
        for group in groups:
            for i in group:
                gather_copy(s, b, i).start()

    def arrived(s, b, *groups):
        for group in groups:
            for i in group:
                gather_copy(s, b, i).wait_recv()

    def pack_copy(s, b, i):
        up, down, across = at(dz=1), at(dz=-1), at(other=1)
        here, there, target = [
            (0, 1, across), (0, 3, up), (0, 2, down),
            ((3, 6, up), (2, 6, down))[b],
            (1, 5, up), (1, 4, down),
            (6, 7, across),
        ][i]
        return pltpu.make_async_remote_copy(
            src_ref=packs.at[s, here, b],
            dst_ref=packs.at[s, there, b],
            send_sem=pack_send.at[s, b, i],
            recv_sem=pack_recv.at[s, b, i],
            device_id=target,
            device_id_type=MESH,
        )

    PACK_OWN, PACK_AHEAD, PACK_ROUND, PACK_CROSS = (1, 2, 0), (3,), (4, 5), (6,)

    def pack_send_on(s, b, *groups):
        for group in groups:
            for i in group:
                pack_copy(s, b, i).start()

    def pack_arrived(s, b, *groups):
        for group in groups:
            for i in group:
                pack_copy(s, b, i).wait_recv()

    def own_band(s, b):
        lo, _, hi = bounds(s, b)
        gathered[s, 0, pl.ds(lo, hi - lo), :] = hid_p[pl.ds(lo, hi - lo), :].astype(BF)

    def relay(q):
        def unit(u, _):
            tap = u % 9
            spread[...] = raw[2 * q + u // 9, tap + odd * (6 - 6 * (tap // 3))].astype(F32)
            for g in range(4):
                wts[q, pl.ds(pl.multiple_of(u * 128, 128), 128), pl.ds(g * 128, 128)] = spread[
                    pl.ds(g, 128, stride=4), :
                ].astype(BF)
            return 0

        lax.fori_loop(0, 18, unit, 0)

    def relay_input():
        for dy in range(3):
            for dx in range(3):
                spread[pl.ds(0, 256), :] = raw_in[3 * (dy + odd * (2 - 2 * dy)) + dx].astype(F32)
                for g in range(4):
                    wts_in[pl.ds(dy * 256 + dx * 64, 64), pl.ds(g * 128, 128)] = spread[
                        pl.ds(g, 64, stride=4), :
                    ].astype(BF)
            wts_in[pl.ds(dy * 256 + 192, 64), :] = jnp.zeros((64, 512), BF)

    def frames_part(s, b):
        lo, count = ((0, DONE[s]), (DONE[s], OUT_ROWS - DONE[s]))[b]
        lhs = jnp.concatenate(
            [
                fr_pair[s, pl.ds(lo + dy * PITCH + dx, count), :].astype(BF)
                for dy in range(3)
                for dx in (0, 2)
            ],
            axis=1,
        )
        total[pl.ds(lo, count), :] = jnp.dot(lhs, wts_in[...], preferred_element_type=F32)

    def hidden_part(s, b, q):
        lo, count = ((0, DONE[s]), (DONE[s], OUT_ROWS - DONE[s]))[b]
        reach = (SENT[s], PAD_ROWS - DONE[s])[b]
        for p in range(2):
            window[p, pl.ds(0, reach), :] = gathered[s, 2 * q + p, pl.ds(lo, reach), :].astype(F32)
            pack_f[p] = packs[s, 2 * q + p, b].astype(F32)
            for x, slot in ((0, 0), (PITCH - 1, CELLS)):
                ys = [y for y in range(*column(b)) if lo <= PITCH * (y + 1) + x < min(lo + count + 78, PAD_ROWS)]
                window[p, pl.ds(PITCH * (ys[0] + 1) + x - lo, len(ys), stride=PITCH), :] = pack_f[
                    p, pl.ds(slot + ys[0] - column(b)[0], len(ys)), :
                ]
            if b == 1:
                window[p, pl.ds(PITCH * PITCH - lo, PAD_ROWS - PITCH * PITCH), :] = jnp.zeros(
                    (PAD_ROWS - PITCH * PITCH, 128), F32
                )
            window[p, pl.ds((0, PITCH * (PITCH - 1) - lo)[b], PITCH), :] = pack_f[
                p, pl.ds(2 * CELLS, PITCH), :
            ]
        lhs = jnp.concatenate(
            [window[p, pl.ds(tap, count), :].astype(BF) for p in range(2) for tap in TAPS], axis=1
        )
        total[pl.ds(lo, count), :] += jnp.dot(lhs, wts[q], preferred_element_type=F32)

    def gates_part(s, b):
        lo, count = ((0, DONE[s]), (DONE[s], OUT_ROWS - DONE[s]))[b]
        tile = TILES[s][b]

        def one(i, _):
            first = pl.multiple_of(lo + i * tile, 8)
            gate = [
                total[pl.ds(first, tile), pl.ds(g * 128, 128)] + bias_v[pl.ds(g, 1), :]
                for g in range(4)
            ]
            new = sigmoid(gate[1]) * cell[pl.ds(first, tile), :] + sigmoid(gate[0]) * jnp.tanh(gate[3])
            cell[pl.ds(first, tile), :] = new
            if s == 0:
                hid_p[pl.ds(first + PITCH + 1, tile), :] = sigmoid(gate[2]) * jnp.tanh(new)
            else:
                hid_f[pl.ds(first, tile), :] = sigmoid(gate[2]) * jnp.tanh(new)
            return 0

        lax.fori_loop(0, count // tile, one, 0)

    both = (hid_p, fr_p)
    own_band(0, 0)
    halo_fill(0, None, both)
    own_band(0, 1)
    pl.semaphore_wait(barrier, len(partners))
    halo_start(0, None)
    send(0, 0, FIRST, SECOND)
    loads[2].wait()
    relay_input()

    lane = lax.broadcasted_iota(jnp.int32, (104, 128), 1)

    def pair_up(i, _):
        first = pl.multiple_of(i * 104, 8)
        here = fr_p[pl.ds(first, 104), :]
        there = fr_p[pl.ds(first + 1, 104), :]
        fr_pair[0, pl.ds(first, 104), :] = jnp.where(lane < 64, here, pltpu.roll(there, 64, 1))
        fr_pair[1, pl.ds(first, 104), :] = jnp.where(lane < 64, pltpu.roll(here, 64, 1), there)
        return 0

    cell[...] = jnp.zeros_like(cell)
    loads[11].wait()
    loads[12].wait()
    for y in range(ROWS):
        cell[pl.ds(PITCH * y, ROWS), :] = cell_v[y_of(y)]
    for j in range(8):
        loads[3 + j].wait()
    def finish(b):
        lo, count = ((0, DONE[1]), (DONE[1], OUT_ROWS - DONE[1]))[b]
        rows = pl.ds(lo, count)
        copies = [
            pltpu.make_async_copy(hid_f.at[rows], hid_out.at[rows], store_sem.at[0, b]),
            pltpu.make_async_copy(cell.at[rows], cell_out.at[rows], store_sem.at[1, b]),
        ]
        for copy in copies:
            copy.start()
        return copies

    relay(0)
    halo_finish(0, 0, None)
    pack_send_on(0, 0, PACK_OWN)
    pack_send_on(0, 1, PACK_OWN)
    send(0, 1, FIRST, SECOND)
    frames_halo()
    lax.fori_loop(0, PAD_ROWS // 104, pair_up, 0)
    relay(1)
    relay(2)
    relay(3)

    arrived(0, 0, FIRST, SECOND)
    send(0, 0, AHEAD, TAILS)
    pack_arrived(0, 0, PACK_OWN)
    pack_send_on(0, 0, PACK_AHEAD, PACK_ROUND)
    send(0, 0, ROUND)
    frames_part(0, 0)
    hidden_part(0, 0, 0)
    pack_arrived(0, 1, PACK_OWN)
    pack_send_on(0, 1, PACK_AHEAD, PACK_ROUND)
    arrived(0, 0, AHEAD)
    send(0, 0, CROSS)
    pack_arrived(0, 0, PACK_AHEAD)
    pack_send_on(0, 0, PACK_CROSS)
    hidden_part(0, 0, 1)
    arrived(0, 1, FIRST, SECOND)
    send(0, 1, AHEAD, TAILS, ROUND)
    frames_part(0, 1)
    hidden_part(0, 1, 0)
    arrived(0, 0, ROUND, TAILS)
    pack_arrived(0, 0, PACK_ROUND)
    hidden_part(0, 0, 2)
    arrived(0, 1, AHEAD)
    send(0, 1, CROSS)
    pack_arrived(0, 1, PACK_AHEAD)
    pack_send_on(0, 1, PACK_CROSS)
    arrived(0, 0, CROSS)
    pack_arrived(0, 0, PACK_CROSS)
    hidden_part(0, 0, 3)
    gates_part(0, 0)
    halo_fill(1, 0, (hid_p,))
    halo_start(1, 0)
    own_band(1, 0)
    send(1, 0, FIRST, SECOND)
    hidden_part(0, 1, 1)
    arrived(0, 1, ROUND, TAILS)
    pack_arrived(0, 1, PACK_ROUND)
    hidden_part(0, 1, 2)
    halo_finish(1, 1, 0)
    pack_send_on(1, 0, PACK_OWN)
    arrived(0, 1, CROSS)
    pack_arrived(0, 1, PACK_CROSS)
    hidden_part(0, 1, 3)
    arrived(1, 0, FIRST, SECOND)
    send(1, 0, AHEAD, TAILS)
    gates_part(0, 1)
    halo_fill(2, 1, (hid_p,))
    halo_start(2, 1)
    own_band(1, 1)
    send(1, 1, FIRST, SECOND)

    pack_arrived(1, 0, PACK_OWN)
    pack_send_on(1, 0, PACK_AHEAD, PACK_ROUND)
    frames_part(1, 0)
    hidden_part(1, 0, 0)
    halo_finish(2, 1, 1)
    pack_send_on(1, 1, PACK_OWN)
    send(1, 0, ROUND)
    arrived(1, 0, AHEAD)
    send(1, 0, CROSS)
    hidden_part(1, 0, 1)
    pack_arrived(1, 0, PACK_AHEAD)
    pack_send_on(1, 0, PACK_CROSS)
    arrived(1, 1, FIRST, SECOND)
    send(1, 1, AHEAD, TAILS)
    pack_arrived(1, 1, PACK_OWN)
    pack_send_on(1, 1, PACK_AHEAD, PACK_ROUND)
    send(1, 1, ROUND)
    frames_part(1, 1)
    hidden_part(1, 1, 0)
    arrived(1, 0, ROUND, TAILS)
    pack_arrived(1, 0, PACK_ROUND)
    hidden_part(1, 0, 2)
    arrived(1, 1, AHEAD)
    send(1, 1, CROSS)
    pack_arrived(1, 1, PACK_AHEAD)
    pack_send_on(1, 1, PACK_CROSS)
    arrived(1, 0, CROSS)
    pack_arrived(1, 0, PACK_CROSS)
    hidden_part(1, 0, 3)
    gates_part(1, 0)
    ends = finish(0)
    hidden_part(1, 1, 1)
    arrived(1, 1, ROUND, TAILS)
    pack_arrived(1, 1, PACK_ROUND)
    hidden_part(1, 1, 2)
    arrived(1, 1, CROSS)
    pack_arrived(1, 1, PACK_CROSS)
    hidden_part(1, 1, 3)
    gates_part(1, 1)
    ends += finish(1)

    for k in range(8):
        halo_copy(0, k, False).wait_send()
    for b in range(2):
        for k in sides(b):
            halo_copy(1 + b, k, False).wait_send()
    for s in range(2):
        for b in range(2):
            for i in range(14):
                gather_copy(s, b, i).wait_send()
            for i in range(7):
                pack_copy(s, b, i).wait_send()
    for copy in ends:
        copy.wait()


def lay_out(hid_in, cell_in, hid_out, cell_out):
    odd = lax.axis_index("sy") % 2
    for r in range(ROWS):
        y = r + odd * (ROWS - 1 - 2 * r)
        hid_out[y] = hid_in[pl.ds(PITCH * r, ROWS), :].astype(BF)
        cell_out[y] = cell_in[pl.ds(PITCH * r, ROWS), :]


def per_device(frames, w_input, w_hidden, biases, hidden_init, cell_init):
    w_in = w_input.reshape(9, 256, 128)
    w_hid = w_hidden.reshape(9, 4096, 128)
    dma = pltpu.SemaphoreType.DMA
    flat = pl.pallas_call(
        kernel,
        out_shape=(jax.ShapeDtypeStruct((OUT_ROWS, 128), F32),) * 2,
        in_specs=[pl.BlockSpec(memory_space=pl.ANY)] * 6,
        out_specs=(pl.BlockSpec(memory_space=pl.ANY),) * 2,
        scratch_shapes=[
            pltpu.VMEM((ROWS, ROWS, 128), BF),
            pltpu.VMEM((ROWS, ROWS, 128), BF),
            pltpu.VMEM((ROWS, ROWS, 128), F32),
            pltpu.VMEM((4, 128), F32),
            pltpu.VMEM((9, 256, 128), BF),
            pltpu.VMEM((8, 9, 512, 128), BF),
            pltpu.VMEM((4, 2304, 512), BF),
            pltpu.VMEM((768, 512), BF),
            pltpu.VMEM((512, 128), F32),
            pltpu.VMEM((PAD_ROWS + 8, 128), F32),
            pltpu.VMEM((PAD_ROWS + 8, 128), F32),
            pltpu.VMEM((2, PAD_ROWS, 128), F32),
            pltpu.VMEM((2, 8, PAD_ROWS, 128), BF),
            pltpu.VMEM((2, SENT[0], 128), F32),
            pltpu.VMEM((OUT_ROWS, 512), F32),
            pltpu.VMEM((OUT_ROWS, 128), F32),
            pltpu.VMEM((3, 8, 2, STRIP, 128), BF),
            pltpu.VMEM((3, 8, 2, STRIP, 128), BF),
            pltpu.VMEM((OUT_ROWS, 128), F32),
            pltpu.VMEM((2, 8, 2, 80, 128), BF),
            pltpu.VMEM((2, 80, 128), F32),
            dma((13,)),
            dma((3, 8)),
            dma((3, 8)),
            dma((2, 2, 14)),
            dma((2, 2, 14)),
            dma((2, 2, 7)),
            dma((2, 2, 7)),
            dma((2, 2)),
        ],
        compiler_params=pltpu.CompilerParams(
            collective_id=0, has_side_effects=True, vmem_limit_bytes=60 * 1024 * 1024
        ),
        name="conv_lstm",
    )(frames, w_in, w_hid, biases, hidden_init, cell_init)
    return pl.pallas_call(
        lay_out,
        out_shape=(
            jax.ShapeDtypeStruct((ROWS, ROWS, 128), BF),
            jax.ShapeDtypeStruct((ROWS, ROWS, 128), F32),
        ),
        in_specs=[pl.BlockSpec(memory_space=pltpu.VMEM)] * 2,
        out_specs=(pl.BlockSpec(memory_space=pltpu.VMEM),) * 2,
        name="lay_out",
    )(*flat)


def solution(mesh):
    in_specs = (
        P("sy", "sx", None),
        P(None, None, None, "ch"),
        P(None, None, None, "ch"),
        P(None, "ch"),
        P("sy", "sx", "ch"),
        P("sy", "sx", "ch"),
    )
    out_specs = (P("sy", "sx", "ch"), P("sy", "sx", "ch"))
    return jax.shard_map(
        per_device, mesh=mesh, in_specs=in_specs, out_specs=out_specs, check_vma=False
    )
```
